128 devices in a mesh: mom: 8 (over x, core), tm: 16 (over z, y).
Axes of the slice: x: 4, y: 4, z: 4, core: 2. Of those that a mesh axis runs over, the one named last changes fastest.
Arguments:
- hist_less: bfloat16 [2, 64, 2048, 2048], P(None, 'mom', None, 'tm'), may hold values from -6 to 6
- hist_great: bfloat16 [2, 64, 2048, 2048], P(None, 'mom', None, 'tm'), may hold values from -6 to 6
- row_less: float32 [2, 64, 2048], P(None, 'mom', 'tm'), may hold values from -6 to 6
- row_great: float32 [2, 64, 2048], P(None, 'mom', 'tm'), may hold values from -6 to 6
- mom_table: int32 [64], replicated, may hold values from 0 to 63, each once
Outputs:
- out_less: float32 [2, 64, 2048], P(None, 'mom', 'tm')
- out_great: float32 [2, 64, 2048], P(None, 'mom', 'tm')
The draws below stay inside these ranges and needn't reach their ends.
Inputs may be any that keep to these rules, and one draw needn't show every extreme that they name: `mom_table`: each slot holds a different lattice momentum.
All inputs are finite; a program needn't handle non-finite values.
Results may differ from the reference program's by a relative error of at most 0.004.
Values may be sent and summed in bfloat16 or wider, within the bound.
A program may use at most 128 MiB of HBM per device.

```python
import math
import jax
import jax.numpy as jnp
from jax import lax

LSIDE = 8
K = 64
TIMES = 2048
NEW = 2
PASS = 2


def shard_levels(rng, dims, cuts, least, high):
    def one(position, shards_of):
        heights = jax.random.uniform(jax.random.fold_in(jax.random.fold_in(rng, 6), position), (shards_of,), jnp.float32, least / len(cuts), high / len(cuts))
        return jnp.repeat(jnp.exp(heights), dims[position] // shards_of).reshape((-1,) + (1,) * (len(dims) - position - 1))

    factor_of = one(*cuts[0])
    for cut in cuts[1:]:
        factor_of = factor_of * one(*cut)
    return factor_of


def centred(own_key, extent, deviation, most, pieces=(), kind=jnp.bfloat16):
    level = shard_levels(own_key, extent, pieces, -0.22, 0.18) if pieces else 1.0
    entries = jax.random.normal(own_key, extent, jnp.float32) * deviation * level
    return jnp.minimum(jnp.maximum(entries, -most), most).astype(kind)


def setup_inputs(seed: int = 0) -> dict:
    key_of = jax.random.split(jax.random.key(seed), 6)
    hist_less = centred(key_of[0], (2, K, TIMES, TIMES), 1.0, 6.0, ((1, 8), (3, 16)))
    hist_great = centred(key_of[1], (2, K, TIMES, TIMES), 1.0, 6.0, ((1, 8), (3, 16)))
    row_less = centred(key_of[2], (2, K, TIMES), 1.0, 6.0, ((1, 8), (2, 16)), jnp.float32)
    row_great = centred(key_of[3], (2, K, TIMES), 1.0, 6.0, ((1, 8), (2, 16)), jnp.float32)
    mom_table = jax.random.permutation(key_of[4], K).astype(jnp.int32)
    return dict(hist_less=hist_less, hist_great=hist_great, row_less=row_less, row_great=row_great, mom_table=mom_table)


coupling = 1.0
time_step = 0.08


def tables(mom_table, side):
    mom_x = (mom_table // side).astype(jnp.float32)
    mom_y = (mom_table % side).astype(jnp.float32)
    site_index = jnp.arange(side * side, dtype=jnp.int32)
    site_x = (site_index // side).astype(jnp.float32)
    site_y = (site_index % side).astype(jnp.float32)
    factor = 2.0 * math.pi / side
    phase_grid = factor * (site_x[:, None] * mom_x[None, :] + site_y[:, None] * mom_y[None, :])
    energy = -2.0 * (jnp.cos(factor * mom_x) + jnp.cos(factor * mom_y))
    return jnp.cos(phase_grid), jnp.sin(phase_grid), energy


def self_energy(current, cos_tab, sin_tab):
    count = current.shape[2]
    high = lax.Precision.HIGHEST

    def forward(table, block):
        return jnp.einsum('rk,akp->arp', table, block, precision=high)

    def backward(table, block):
        return jnp.einsum('rk,arp->akp', table, block, precision=high)

    real_part, imag_part = current[0], current[1]
    g_real = (forward(cos_tab, real_part) - forward(sin_tab, imag_part)) / count
    g_imag = (forward(sin_tab, real_part) + forward(cos_tab, imag_part)) / count
    less_real, less_imag = g_real[0], g_imag[0]
    great_real, great_imag = g_real[1], g_imag[1]
    scale = -coupling * coupling
    less_sq_real = less_real * less_real - less_imag * less_imag
    less_sq_imag = 2.0 * less_real * less_imag
    great_sq_real = great_real * great_real - great_imag * great_imag
    great_sq_imag = 2.0 * great_real * great_imag
    sig_less_real = scale * (less_sq_real * great_real + less_sq_imag * great_imag)
    sig_less_imag = scale * (less_sq_imag * great_real - less_sq_real * great_imag)
    sig_great_real = scale * (great_sq_real * less_real + great_sq_imag * less_imag)
    sig_great_imag = scale * (great_sq_imag * less_real - great_sq_real * less_imag)
    site_real = jnp.stack([sig_less_real, sig_great_real])
    site_imag = jnp.stack([sig_less_imag, sig_great_imag])
    out_real = backward(cos_tab, site_real) + backward(sin_tab, site_imag)
    out_imag = backward(cos_tab, site_imag) - backward(sin_tab, site_real)
    return jnp.stack([out_real, out_imag])


def exact_sum(vector, matrix):
    prods = jnp.einsum('cks,dksu->cdku', vector.astype(jnp.float32), matrix.astype(jnp.float32),
                       precision=lax.Precision.HIGHEST)
    return jnp.stack([prods[0, 0] - prods[1, 1], prods[0, 1] + prods[1, 0]])


def contract(sigma, h_less, h_great, mask, summer):
    below = mask[None, None]
    swapped = jnp.where(below, h_great, h_less)
    kept = jnp.where(below, h_less, h_great)
    sig_less = sigma[:, 0]
    sig_great = sigma[:, 1]
    lesser = summer(sig_great, h_less) - summer(sig_less, swapped)
    greater = summer(sig_great, kept) - summer(sig_less, h_great)
    return jnp.stack([lesser, greater], axis=1)


def integral(sigma, hist_less, hist_great):
    total = hist_less.shape[2]
    index_all = jnp.arange(total, dtype=jnp.int32)
    mask = index_all[:, None] < index_all[None, :]

    def one_mom(slot):
        part_sig = lax.dynamic_slice_in_dim(sigma, slot, 1, 2)
        part_less = lax.dynamic_slice_in_dim(hist_less, slot, 1, 1)
        part_great = lax.dynamic_slice_in_dim(hist_great, slot, 1, 1)
        return contract(part_sig, part_less, part_great, mask, exact_sum)

    out_all = lax.map(one_mom, jnp.arange(sigma.shape[2], dtype=jnp.int32))
    return jnp.moveaxis(out_all[:, :, :, 0, :], 0, 2)


def rotate(values, phases):
    cos_part = jnp.cos(phases)[None, :, None]
    sin_part = jnp.sin(phases)[None, :, None]
    real_part = cos_part * values[0] + sin_part * values[1]
    imag_part = cos_part * values[1] - sin_part * values[0]
    return jnp.stack([real_part, imag_part])


def turn(values):
    return jnp.stack([values[1], -values[0]])


def propagate(current, energy, evaluate):
    memory, density = evaluate(current)
    for index_new in range(NEW):
        phases = (energy + coupling * density) * time_step
        trial = rotate(current + time_step * turn(memory), phases)
        for index_pass in range(PASS):
            memory_new, density_new = evaluate(trial)
            phases = (energy + coupling * 0.5 * (density + density_new)) * time_step
            trial = rotate(current + 0.5 * time_step * turn(memory), phases) + 0.5 * time_step * turn(memory_new)
        current = trial
        if index_new + 1 < NEW:
            memory, density = evaluate(current)
    return current


def reference(hist_less, hist_great, row_less, row_great, mom_table):
    cos_tab, sin_tab, energy = tables(mom_table, LSIDE)

    def evaluate(current):
        last_col = current[:, 0, :, -1]
        density = jnp.sum(last_col * last_col) / K
        sigma = self_energy(current, cos_tab, sin_tab).astype(jnp.bfloat16)
        return integral(sigma, hist_less, hist_great), density

    current = jnp.stack([row_less, row_great], axis=1)
    final = propagate(current, energy, evaluate)
    return final[:, 0], final[:, 1]
```

```python
import functools
import math

import jax
import jax.numpy as jnp
from jax import lax
from jax.experimental import pallas as pl
from jax.experimental.pallas import tpu as pltpu
from jax.sharding import PartitionSpec as P

LSIDE = 8
K = 64
NEW = 2
PASS = 2
COUPLING = 1.0
STEP = 0.08
MESH = pl.DeviceIdType.MESH
F32 = jnp.float32
BF16 = jnp.bfloat16
MOMS = 8
SHARDS = 16
OWN = 8
COLS = 128
STAGES = PASS + 1
EVALS = NEW * STAGES


def eighth_cos(index):
    index = index & 7
    root = math.sqrt(0.5)
    odd = jnp.where((index == 1) | (index == 7), root, -root)
    even = jnp.where(index == 0, 1.0, jnp.where(index == 4, -1.0, 0.0))
    return jnp.where((index & 1) == 1, odd, even).astype(F32)


def eighth_sin(index):
    return eighth_cos(index + 6)


def halves(values):
    high = values.astype(BF16)
    return high, (values - high.astype(F32)).astype(BF16)


def dot(left, right):
    return jnp.dot(left, right, preferred_element_type=F32)


def iota(shape, dim):
    return lax.broadcasted_iota(jnp.int32, shape, dim)


def kernel(
    hist_less, hist_great, row_less, row_great, mom_table,
    out_less, out_great,
    hist, forward, backward, rows, sig, coeff, state, memory, energy, density,
    hist_sem, row_send, row_recv, sig_send, sig_recv,
):
    mom_pos = lax.axis_index("mom")
    time_pos = lax.axis_index("tm")
    times = SHARDS * COLS

    def history_copies():
        for which, source in enumerate((hist_less, hist_great)):
            for part in range(2):
                yield pltpu.make_async_copy(
                    source.at[part],
                    hist.at[which, part, :, pl.ds(0, times), :],
                    hist_sem.at[which, part],
                )

    for copy in history_copies():
        copy.start()

    barrier = pltpu.get_barrier_semaphore()
    for shift in range(1, MOMS):
        pl.semaphore_signal(
            barrier, inc=1, device_id={"mom": lax.rem(mom_pos + shift, MOMS)}, device_id_type=MESH
        )
    for shift in range(1, SHARDS):
        pl.semaphore_signal(
            barrier, inc=1, device_id={"tm": lax.rem(time_pos + shift, SHARDS)}, device_id_type=MESH
        )

    lane = iota((1, 128), 1)
    lane_slot = (lane >> 4) * 8 + (lane & 7)
    lane_mom = jnp.zeros((1, 128), jnp.int32)
    for slot in range(K):
        lane_mom = jnp.where(lane_slot == slot, mom_table[slot], lane_mom)
    site = iota((128, 128), 0) & 63
    is_imag_row = iota((128, 128), 0) >= 64
    is_imag_col = (iota((128, 128), 1) & 8) != 0
    angle = (site >> 3) * (lane_mom >> 3) + (site & 7) * (lane_mom & 7)
    cos_part, sin_part = eighth_cos(angle), eighth_sin(angle)
    table = jnp.where(
        is_imag_row == is_imag_col, cos_part, jnp.where(is_imag_row, sin_part, -sin_part)
    ) * (1.0 / K)
    high, low = halves(table)
    forward[:, 0:128] = high
    forward[:, 128:256] = high
    forward[:, 256:384] = low

    row_id = iota((32, 1), 0)
    row_slot = (row_id >> 3) * 2 + (row_id & 1)
    own_id = iota((OWN, 1), 0)
    row_mom = jnp.zeros((32, 1), jnp.int32)
    own_mom = jnp.zeros((OWN, 1), jnp.int32)
    for slot in range(OWN):
        value = mom_table[mom_pos * OWN + slot]
        row_mom = jnp.where(row_slot == slot, value, row_mom)
        own_mom = jnp.where(own_id == slot, value, own_mom)
    col = iota((32, 128), 1)
    site = col & 63
    angle = (site >> 3) * (row_mom >> 3) + (site & 7) * (row_mom & 7)
    cos_part, sin_part = eighth_cos(angle), eighth_sin(angle)
    is_imag_row = (iota((32, 128), 0) & 2) != 0
    is_imag_col = col >= 64
    table = jnp.where(
        is_imag_row == is_imag_col, cos_part, jnp.where(is_imag_row, -sin_part, sin_part)
    ) * (-COUPLING * COUPLING)
    high, low = halves(table)
    backward[:, 0:128] = high
    backward[:, 128:256] = high
    backward[:, 256:384] = low

    energy[...] = jnp.broadcast_to(
        -2.0 * (eighth_cos(own_mom >> 3) + eighth_cos(own_mom & 7)), (OWN, COLS)
    )
    sub = iota((OWN, COLS), 0)

    def publish(slot, real_less, imag_less, real_great, imag_great):
        for comp, pair in enumerate(((real_less, imag_less), (real_great, imag_great))):
            high, low = halves(jnp.concatenate(pair, axis=0))
            rows[slot, mom_pos, 0, comp] = high
            rows[slot, mom_pos, 1, comp] = low

    for part in range(2):
        state[part, 0] = row_less[part]
        state[part, 1] = row_great[part]
    publish(0, row_less[0], row_less[1], row_great[0], row_great[1])

    pl.semaphore_wait(barrier, MOMS + SHARDS - 2)

    def send_row(slot, shift):
        return pltpu.make_async_remote_copy(
            src_ref=rows.at[slot, mom_pos],
            dst_ref=rows.at[slot, mom_pos],
            send_sem=row_send.at[shift],
            recv_sem=row_recv.at[slot, shift],
            device_id={"mom": lax.rem(mom_pos + shift, MOMS)},
            device_id_type=MESH,
        )

    def send_sigma(slot, shift, extent):
        return pltpu.make_async_remote_copy(
            src_ref=sig.at[slot, time_pos, pl.ds(0, extent), :],
            dst_ref=sig.at[slot, time_pos, pl.ds(0, extent), :],
            send_sem=sig_send.at[shift],
            recv_sem=sig_recv.at[slot, shift],
            device_id={"tm": lax.rem(time_pos + shift, SHARDS)},
            device_id_type=MESH,
        )

    def self_energy(slot):
        stacked = [
            jnp.concatenate(
                [rows[slot, :, half, comp].reshape(128, COLS) for comp in range(2)], axis=1
            )
            for half in range(2)
        ]
        total = jnp.zeros((OWN, COLS), F32)
        for owner in range(MOMS):
            less = rows[slot, owner, 0, 0].astype(F32) + rows[slot, owner, 1, 0].astype(F32)
            total = total + less[0:8] * less[0:8] + less[8:16] * less[8:16]
        last = jnp.sum(
            jnp.where(iota((OWN, COLS), 1) == COLS - 1, total, 0.0), axis=(0, 1), keepdims=True
        ) * (1.0 / K)
        last = jnp.broadcast_to(last, (OWN, COLS))
        high = last.astype(BF16).astype(F32)
        middle = (last - high).astype(BF16).astype(F32)
        low = last - high - middle
        note = jnp.concatenate([high, jnp.where(sub < 4, middle, low)], axis=0).astype(BF16)

        site = dot(forward[...], jnp.concatenate([stacked[0], stacked[1], stacked[0]], axis=0))
        less_re, less_im = site[0:64, 0:128], site[64:128, 0:128]
        great_re, great_im = site[0:64, 128:256], site[64:128, 128:256]
        less_sq_re = less_re * less_re - less_im * less_im
        less_sq_im = 2.0 * less_re * less_im
        great_sq_re = great_re * great_re - great_im * great_im
        great_sq_im = 2.0 * great_re * great_im
        sigma_re = jnp.concatenate(
            [less_sq_re * great_re + less_sq_im * great_im, great_sq_re * less_re + great_sq_im * less_im],
            axis=1,
        )
        sigma_im = jnp.concatenate(
            [less_sq_im * great_re - less_sq_re * great_im, great_sq_im * less_re - great_sq_re * less_im],
            axis=1,
        )
        high, low = halves(jnp.concatenate([sigma_re, sigma_im], axis=0))
        both = dot(backward[...], jnp.concatenate([high, low, high], axis=0))
        is_less = (iota((32, COLS), 0) & 4) != 0
        own = jnp.where(is_less, both[:, 0:128], both[:, 128:256])
        sig[slot, time_pos, 0:32, :] = own.astype(BF16)
        sig[slot, time_pos, 32:48, :] = note

    def split_diagonal():
        start = pl.multiple_of(time_pos * COLS, COLS)
        below = (iota((COLS, COLS), 0) < iota((COLS, COLS), 1)).astype(F32).astype(BF16)
        above = (iota((COLS, COLS), 0) >= iota((COLS, COLS), 1)).astype(F32).astype(BF16)

        def one(slot, carry):
            for which in range(2):
                for part in range(2):
                    block = hist[which, part, slot, pl.ds(start, COLS), :]
                    hist[which, part, slot, pl.ds(start, COLS), :] = block * below
                    hist[which, part, slot, pl.ds(times, COLS), :] = block * above
            return carry

        lax.fori_loop(0, OWN, one, 0)

    def contract(slot):
        for block in range(SHARDS + 1):
            if block < SHARDS:
                piece = sig[slot, block, 0:32, :].astype(F32)
                on_below = jnp.where(block <= time_pos, 1.0, 0.0).astype(F32)
                on_above = 1.0 - on_below
                lower, upper = piece * on_below, piece * on_above
            else:
                upper = sig[slot, time_pos, 0:32, :].astype(F32)
                lower = jnp.zeros_like(upper)
            for pair in range(4):
                span = slice(8 * pair, 8 * pair + 8)
                coeff[pair, :, block * COLS : (block + 1) * COLS] = jnp.concatenate(
                    [lower[span], upper[span]], axis=0
                ).astype(BF16)

        even = (sub & 1) == 0
        greater = sub < 4
        real = (sub & 2) == 0
        found = [[jnp.zeros((OWN, COLS), F32) for _ in range(2)] for _ in range(2)]
        for pair in range(4):
            left = coeff[pair]
            sums = []
            for which in range(2):
                products = []
                for parity in range(2):
                    slot_of = 2 * pair + parity
                    right = jnp.concatenate([hist[which, 0, slot_of], hist[which, 1, slot_of]], axis=1)
                    products.append(dot(left, right))
                sums.append(
                    [
                        [
                            jnp.where(
                                even,
                                products[0][8 * side : 8 * side + 8, part * 128 : part * 128 + 128],
                                products[1][8 * side : 8 * side + 8, part * 128 : part * 128 + 128],
                            )
                            for part in range(2)
                        ]
                        for side in range(2)
                    ]
                )
            less, great = sums
            for comp, upper in enumerate((less, great)):
                mixed = [
                    jnp.where(greater, less[0][part] + upper[1][part], -(great[0][part] + upper[1][part]))
                    for part in range(2)
                ]
                for part, term in enumerate(
                    (jnp.where(real, mixed[0], -mixed[1]), jnp.where(real, mixed[1], mixed[0]))
                ):
                    term = term + pltpu.roll(term, 4, 0)
                    term = term + pltpu.roll(term, 2, 0)
                    found[comp][part] = jnp.where((sub >> 1) == pair, term, found[comp][part])
        return found

    def evaluation(index, carry):
        slot = index & 1
        stage = lax.rem(index, STAGES)
        predict = stage == 0
        for shift in range(1, MOMS):
            send_row(slot, shift).start()
        for shift in range(1, MOMS):
            send_row(slot, shift).wait()
        self_energy(slot)

        @pl.when(time_pos == SHARDS - 1)
        def _():
            for shift in range(1, SHARDS):
                send_sigma(slot, shift, 48).start()

        @pl.when(time_pos != SHARDS - 1)
        def _():
            for shift in range(1, SHARDS):
                send_sigma(slot, shift, 32).start()

        @pl.when(index == 0)
        def _():
            for copy in history_copies():
                copy.wait()
            split_diagonal()

        @pl.when(time_pos == SHARDS - 1)
        def _():
            for shift in range(1, SHARDS):
                send_sigma(slot, shift, 48).wait_send()

        @pl.when(time_pos != SHARDS - 1)
        def _():
            for shift in range(1, SHARDS):
                send_sigma(slot, shift, 32).wait_send()

        for shift in range(1, SHARDS):
            source = lax.rem(time_pos + SHARDS - shift, SHARDS)

            @pl.when(source == SHARDS - 1)
            def _():
                send_sigma(slot, shift, 48).wait_recv()

            @pl.when(source != SHARDS - 1)
            def _():
                send_sigma(slot, shift, 32).wait_recv()

        found = contract(slot)

        note = sig[slot, SHARDS - 1, 32:48, :].astype(F32)
        now = note[0:8] + (note[8:16] + pltpu.roll(note[8:16], 4, 0))
        before = jnp.where(predict, now, density[...])
        density[...] = before
        phase = (energy[...] + COUPLING * 0.5 * (before + now)) * STEP
        cos_part, sin_part = jnp.cos(phase), jnp.sin(phase)
        first_scale = jnp.where(predict, STEP, 0.5 * STEP).astype(F32)
        fresh = []
        for comp in range(2):
            re_now, im_now = found[comp]
            re_before = jnp.where(predict, re_now, memory[0, comp])
            im_before = jnp.where(predict, im_now, memory[1, comp])
            memory[0, comp] = re_before
            memory[1, comp] = im_before
            re_base = state[0, comp] + first_scale * im_before
            im_base = state[1, comp] - first_scale * re_before
            re_next = cos_part * re_base + sin_part * im_base
            im_next = cos_part * im_base - sin_part * re_base
            fresh.append(jnp.where(predict, re_next, re_next + 0.5 * STEP * im_now))
            fresh.append(jnp.where(predict, im_next, im_next - 0.5 * STEP * re_now))
        publish(1 - slot, *fresh)

        @pl.when(stage == STAGES - 1)
        def _():
            for comp in range(2):
                for part in range(2):
                    state[part, comp] = fresh[2 * comp + part]

        return carry

    lax.fori_loop(0, EVALS, evaluation, 0)
    for part in range(2):
        out_less[part] = state[part, 0]
        out_great[part] = state[part, 1]


def per_device(hist_less, hist_great, row_less, row_great, mom_table):
    vmem = pl.BlockSpec(memory_space=pltpu.VMEM)
    hbm = pl.BlockSpec(memory_space=pltpu.MemorySpace.HBM)
    moms, cols = row_less.shape[1:]
    times = hist_less.shape[2]
    assert (moms, cols, times) == (OWN, COLS, SHARDS * COLS)
    return pl.pallas_call(
        kernel,
        out_shape=[jax.ShapeDtypeStruct(row_less.shape, F32)] * 2,
        in_specs=[hbm, hbm, vmem, vmem, pl.BlockSpec(memory_space=pltpu.SMEM)],
        out_specs=[vmem, vmem],
        scratch_shapes=[
            pltpu.VMEM((2, 2, OWN, times + COLS, COLS), BF16),
            pltpu.VMEM((128, 384), BF16),
            pltpu.VMEM((32, 384), BF16),
            pltpu.VMEM((2, MOMS, 2, 2, 16, COLS), BF16),
            pltpu.VMEM((2, SHARDS, 48, COLS), BF16),
            pltpu.VMEM((4, 16, times + COLS), BF16),
            pltpu.VMEM((2, 2, OWN, COLS), F32),
            pltpu.VMEM((2, 2, OWN, COLS), F32),
            pltpu.VMEM((OWN, COLS), F32),
            pltpu.VMEM((OWN, COLS), F32),
            pltpu.SemaphoreType.DMA((2, 2)),
            pltpu.SemaphoreType.DMA((MOMS,)),
            pltpu.SemaphoreType.DMA((2, MOMS)),
            pltpu.SemaphoreType.DMA((SHARDS,)),
            pltpu.SemaphoreType.DMA((2, SHARDS)),
        ],
        compiler_params=pltpu.CompilerParams(
            collective_id=0, has_side_effects=True, vmem_limit_bytes=56 << 20
        ),
        name="rows",
    )(hist_less, hist_great, row_less, row_great, mom_table)


def solution(mesh):
    placed = (
        P(None, "mom", None, "tm"),
        P(None, "mom", None, "tm"),
        P(None, "mom", "tm"),
        P(None, "mom", "tm"),
        P(),
    )
    assert (mesh.shape["mom"], mesh.shape["tm"]) == (MOMS, SHARDS)
    return jax.shard_map(
        per_device,
        mesh=mesh,
        in_specs=placed,
        out_specs=(P(None, "mom", "tm"), P(None, "mom", "tm")),
        check_vma=False,
    )
```
